32 devices in a mesh: rep: 4 (over y, x), fsdp: 8 (over z, core).
Axes of the slice: x: 2, y: 2, z: 4, core: 2. Of those that a mesh axis runs over, the one named last changes fastest.
Arguments:
- local_params: float32 [4, 8, 1024, 128], P('rep', None, 'fsdp'), may hold values from -7 to 7
- gradients: bfloat16 [4, 8, 1024, 128], P('rep', None, 'fsdp'), may hold values from -200 to 200
- first_moment: float32 [4, 8, 1024, 128], P('rep', None, 'fsdp'), may hold values from -4 to 4
- second_moment: float32 [4, 8, 1024, 128], P('rep', None, 'fsdp'), may hold values from 0.01 to 1
- global_params: float32 [1024, 128], P('fsdp'), may hold values from -6 to 6
- outer_momentum: float32 [1024, 128], P('fsdp'), may hold values from -6 to 6
- fragment_index: int32 [1], replicated, may hold values from 0 to 7
- step_count: int32 [1], replicated, may hold values from 1 to 16
Outputs:
- local_next: float32 [4, 8, 1024, 128], P('rep', None, 'fsdp')
- first_next: float32 [4, 8, 1024, 128], P('rep', None, 'fsdp')
- second_next: float32 [4, 8, 1024, 128], P('rep', None, 'fsdp')
- global_next: float32 [1024, 128], P('fsdp')
- momentum_next: float32 [1024, 128], P('fsdp')
The draws below stay inside these ranges and needn't reach their ends.
All inputs are finite; a program needn't handle non-finite values. Where the reference program divides by a largest or mean magnitude, that divisor is 1e-20 or more.
Results may differ from the reference program's by a relative error of at most 0.0018.
Values may be sent and summed in bfloat16 or wider, within the bound.
A program may use at most 64 MiB of HBM per device.

```python
import math
import jax
import jax.numpy as jnp
from jax import lax

BLOCK = 128
FRAGMENTS = 8
ROWS_DEV = 128
ROWS = 1024
N_REP = 4


def shared_base(key):
    base_key = jax.random.fold_in(key, 7001)
    return jnp.clip(jax.random.normal(base_key, (ROWS, BLOCK), dtype=jnp.float32), -5.0, 5.0)


def draw_local_params(key, part):
    base = shared_base(key)
    drift_key = jax.random.fold_in(key, 7002)
    scale_key = jax.random.fold_in(key, 7003)
    shape = (N_REP, FRAGMENTS, ROWS, BLOCK)
    row_scale = 0.3 * 10.0 ** jax.random.uniform(scale_key, (N_REP, FRAGMENTS, ROWS, 1), dtype=jnp.float32)
    drift = jnp.clip(jax.random.normal(drift_key, shape, dtype=jnp.float32), -4.0, 4.0)
    values = base[None, None] + 0.15 * row_scale * drift
    return values.astype(jnp.float32)


def draw_global_params(key, part):
    base = shared_base(key)
    offset_key = jax.random.fold_in(key, 7005)
    offset = jnp.clip(jax.random.normal(offset_key, (ROWS, BLOCK), dtype=jnp.float32), -4.0, 4.0)
    return (base + 0.05 * offset).astype(jnp.float32)


def draw_gradients(key, part):
    first_key, second_key = jax.random.split(key, 2)
    level_key = jax.random.fold_in(key, 7006)
    shape = (N_REP, FRAGMENTS, ROWS, BLOCK)
    shard_count = ROWS // ROWS_DEV
    shard_level = jax.random.uniform(level_key, (N_REP, shard_count), dtype=jnp.float32)
    row_level = jnp.repeat(shard_level, ROWS_DEV, axis=1)
    trend = jnp.arange(ROWS, dtype=jnp.float32) / max(ROWS - 1, 1)
    row_scale = 10.0 ** (0.4 * trend[None, :] + 0.6 * row_level)
    column_scale = 10.0 ** jax.random.uniform(second_key, (N_REP, FRAGMENTS, 1, BLOCK), dtype=jnp.float32)
    replica_level = jnp.arange(N_REP, dtype=jnp.float32) / max(N_REP - 1, 1)
    replica_scale = 10.0 ** (-1.5 + 2.5 * replica_level) / 20.0
    base = jax.random.normal(first_key, shape, dtype=jnp.float32)
    base = jnp.clip(base, -4.0, 4.0)
    values = base * row_scale[:, None, :, None] * column_scale * replica_scale[:, None, None, None]
    return values.astype(jnp.bfloat16)


def block_levels(own_key, dims, cuts, smallest, top_value):
    loudness, own = 1.0, jax.random.fold_in(own_key, 6)
    for dim, parts in cuts:
        heights = jnp.exp(jax.random.uniform(jax.random.fold_in(own, dim), (parts,), jnp.float32, smallest / len(cuts), top_value / len(cuts)))
        loudness = loudness * jnp.repeat(heights, dims[dim] // parts).reshape([-1 if axis == dim else 1 for axis in range(len(dims))])
    return loudness


def gaussian(key, dims, deviation, reach, cuts=(), kind=jnp.bfloat16):
    drawn = deviation * jax.random.normal(key, dims, jnp.float32)
    if cuts:
        drawn = drawn * block_levels(key, dims, cuts, -0.22, 0.18)
    return jnp.clip(drawn, -reach, reach).astype(kind)


def setup_inputs(seed: int = 0) -> dict:
    seeds = jax.random.split(jax.random.key(seed), 9)
    local_params = draw_local_params(jax.random.fold_in(seeds[8], 71), 0)
    gradients = draw_gradients(jax.random.fold_in(seeds[8], 71), 0)
    first_moment = gaussian(seeds[2], (N_REP, FRAGMENTS, ROWS, BLOCK), 0.3, 4.0, ((0, 4), (2, 8)), jnp.float32)
    second_moment = jnp.clip(jnp.exp(math.log(1.0) - 4.6051702 * jax.random.uniform(seeds[3], (N_REP, FRAGMENTS, ROWS, BLOCK), jnp.float32) ** block_levels(seeds[3], (N_REP, FRAGMENTS, ROWS, BLOCK), ((0, 4), (2, 8)), -0.2, 0.2)), 0.01, 1.0)
    global_params = draw_global_params(jax.random.fold_in(seeds[8], 71), 0)
    outer_momentum = gaussian(seeds[5], (ROWS, BLOCK), 0.5, 6.0, ((0, 8),), jnp.float32)
    fragment_index = jax.random.randint(seeds[6], (1,), 0, FRAGMENTS).astype(jnp.int32)
    step_count = jax.random.randint(seeds[7], (1,), 1, 17).astype(jnp.int32)
    return dict(local_params=local_params, gradients=gradients, first_moment=first_moment, second_moment=second_moment, global_params=global_params, outer_momentum=outer_momentum, fragment_index=fragment_index, step_count=step_count)


def reference(local_params, gradients, first_moment, second_moment, global_params, outer_momentum, fragment_index, step_count):
    grad_float = gradients.astype(jnp.float32)
    square_sum = lax.optimization_barrier(jnp.sum(grad_float * grad_float, axis=(1, 2, 3)))
    threshold = 0.5 * math.sqrt(FRAGMENTS * ROWS * BLOCK)
    clip_factor = jnp.minimum(1.0, threshold / jnp.sqrt(square_sum + 1e-06))
    scaled = grad_float * clip_factor[:, None, None, None]
    first_next = 0.9 * first_moment + 0.1 * scaled
    second_next = 0.95 * second_moment + 0.05 * scaled * scaled
    steps_float = step_count[0].astype(jnp.float32)
    bias_one = 1.0 - 0.9 ** steps_float
    bias_two = 1.0 - 0.95 ** steps_float
    stepped = local_params - 0.1 * (first_next / bias_one / (jnp.sqrt(second_next / bias_two) + 1e-08) + 0.1 * local_params)
    fragment = lax.dynamic_index_in_dim(local_params, fragment_index[0], 1, keepdims=False)
    pseudo = global_params[None] - fragment
    block_scale = (lax.optimization_barrier(jnp.max(jnp.abs(pseudo), axis=2, keepdims=True)) + 1e-06).astype(jnp.bfloat16)
    quantized = (pseudo / block_scale.astype(jnp.float32)).astype(jnp.bfloat16)
    averaged = lax.optimization_barrier(jnp.sum(quantized.astype(jnp.float32) * block_scale.astype(jnp.float32), axis=0)) / N_REP
    momentum_next = 0.9 * outer_momentum + averaged
    global_next = global_params - 0.7 * (averaged + 0.9 * momentum_next)
    stepped_fragment = lax.dynamic_index_in_dim(stepped, fragment_index[0], 1, keepdims=False)
    blended = 0.5 * stepped_fragment + 0.5 * global_next[None]
    selector = (jnp.arange(FRAGMENTS, dtype=jnp.int32) == fragment_index[0])[None, :, None, None]
    local_next = jnp.where(selector, blended[:, None], stepped)
    return (local_next, first_next, second_next, global_next, momentum_next)
```

```python
import functools
import math

import jax
import jax.numpy as jnp
from jax import lax
from jax.experimental import pallas as pl
from jax.experimental.pallas import tpu as pltpu
from jax.sharding import PartitionSpec as P

MESH = pl.DeviceIdType.MESH
SUBLANES = 8
SCALE_ROWS = 16


def read(step_ref, said_ref):
    said_ref[...] = jnp.full(said_ref.shape, step_ref[0].astype(jnp.float32), jnp.float32)


def exchange(
    replicas,
    shards,
    reader,
    frag_ref,
    said_ref,
    p_hbm,
    g_hbm,
    m_hbm,
    v_hbm,
    gp_hbm,
    om_hbm,
    p_ref,
    g_ref,
    m_ref,
    v_ref,
    coef_ref,
    global_ref,
    momentum_ref,
    gp_ref,
    om_ref,
    coded,
    squares,
    load_sems,
    code_send,
    code_recv,
    square_send,
    square_recv,
    code_credit,
    square_credit,
):
    rep = lax.axis_index("rep")
    shard = lax.axis_index("fsdp")
    rows, cols = gp_ref.shape
    fragments = p_ref.shape[1]

    loads = [
        pltpu.make_async_copy(src, dst, load_sems.at[i])
        for i, (src, dst) in enumerate(
            (
                (g_hbm, g_ref),
                (gp_hbm, gp_ref),
                (p_hbm, p_ref),
                (om_hbm, om_ref),
                (m_hbm, m_ref),
                (v_hbm, v_ref),
            )
        )
    ]

    def higher(index, size, act):
        for k in range(1, size):

            @pl.when(index + k < size)
            def _():
                act(index + k)

    def lower(index, size, act):
        for k in range(size - 1, 0, -1):

            @pl.when(index - k >= 0)
            def _():
                act(index - k)

    def signal(sem, **target):
        pl.semaphore_signal(sem, inc=1, device_id=target, device_id_type=MESH)

    def square_copy(source, target):
        return pltpu.make_async_remote_copy(
            src_ref=squares.at[source],
            dst_ref=squares.at[source],
            send_sem=square_send.at[target],
            recv_sem=square_recv.at[source],
            device_id={"fsdp": target},
            device_id_type=MESH,
        )

    def code_copy(source, target):
        return pltpu.make_async_remote_copy(
            src_ref=coded.at[source],
            dst_ref=coded.at[source],
            send_sem=code_send.at[target],
            recv_sem=code_recv.at[source],
            device_id={"rep": target},
            device_id_type=MESH,
        )

    barrier = pltpu.get_barrier_semaphore()
    for load in loads[:3]:
        load.start()
    higher(shard, shards, lambda i: signal(barrier, fsdp=i))
    higher(rep, replicas, lambda i: signal(barrier, rep=i))

    @pl.when(shard + rep > 0)
    def _():
        pl.semaphore_wait(barrier, shard + rep)

    lower(shard, shards, lambda i: signal(square_credit.at[shard], fsdp=i))
    lower(rep, replicas, lambda i: signal(code_credit.at[rep], rep=i))

    eye = lax.broadcasted_iota(jnp.int32, (cols, cols), 0) == lax.broadcasted_iota(
        jnp.int32, (cols, cols), 1
    )

    squares[shard, 1:] = said_ref[...]
    loads[0].wait()
    total = jnp.zeros((SUBLANES, cols), jnp.float32)
    for f in range(fragments):
        grad = g_ref[0, f].astype(jnp.float32)
        total = total + jnp.sum((grad * grad).reshape(-1, SUBLANES, cols), axis=0)
    squares[shard, :1] = jnp.sum(total, axis=0, keepdims=True)
    lower(shard, shards, lambda i: square_copy(shard, i).start())

    for load in loads[1:3]:
        load.wait()
    for load in loads[3:]:
        load.start()
    pseudo = gp_ref[...] - p_ref[0, frag_ref[0]]
    scale = (jnp.max(jnp.abs(pseudo), axis=1, keepdims=True) + 1e-06).astype(jnp.bfloat16)
    scale = scale.astype(jnp.float32)
    coded[rep, :rows] = (pseudo / scale).astype(jnp.bfloat16)
    for c in range(rows // cols):
        column = scale[c * cols : (c + 1) * cols]
        line = jnp.sum(jnp.where(eye, column, 0.0), axis=0, keepdims=True)
        coded[rep, rows + c * SCALE_ROWS : rows + (c + 1) * SCALE_ROWS] = jnp.broadcast_to(
            line, (SCALE_ROWS, cols)
        ).astype(jnp.bfloat16)

    def square_when_heard(i):
        pl.semaphore_wait(square_credit.at[i], 1)
        square_copy(shard, i).start()

    def code_when_heard(i):
        pl.semaphore_wait(code_credit.at[i], 1)
        code_copy(rep, i).start()

    lower(rep, replicas, lambda i: code_copy(rep, i).start())
    higher(rep, replicas, code_when_heard)
    higher(shard, shards, square_when_heard)

    coef_ref[3] = jnp.full((SUBLANES, cols), frag_ref[0].astype(jnp.float32), jnp.float32)
    for load in loads[3:]:
        load.wait()

    for k in range(1, replicas):
        source = lax.rem(rep + k, replicas)
        code_copy(source, source).wait_recv()
    for c in range(rows // cols):
        part = slice(c * cols, (c + 1) * cols)
        summed = jnp.zeros((cols, cols), jnp.float32)
        for r in range(replicas):
            line = coded[r, rows + c * SCALE_ROWS : rows + (c + 1) * SCALE_ROWS]
            line = line.astype(jnp.float32)[:1]
            column = jnp.sum(jnp.where(eye, line, 0.0), axis=1, keepdims=True)
            summed = summed + coded[r, part].astype(jnp.float32) * column
        averaged = summed * (1.0 / replicas)
        momentum = 0.9 * om_ref[part] + averaged
        momentum_ref[part] = momentum
        global_ref[part] = gp_ref[part] - 0.7 * (averaged + 0.9 * momentum)

    def square_heard(source):
        @pl.when(shard != source)
        def _():
            square_copy(source, source).wait_recv()

    square_heard(reader)
    step = jnp.broadcast_to(squares[reader, 1:], (SUBLANES, cols))
    coef_ref[1] = 0.1 / (1.0 - jnp.exp(step * math.log(0.9)))
    coef_ref[2] = 1.0 / (1.0 - jnp.exp(step * math.log(0.95)))
    for s in range(shards):
        if s != reader:
            square_heard(s)
    lanes = squares[0, :1]
    for s in range(1, shards):
        lanes = lanes + squares[s, :1]
    square_sum = jnp.broadcast_to(
        jnp.sum(jnp.broadcast_to(lanes, (SUBLANES, cols)), axis=1, keepdims=True),
        (SUBLANES, cols),
    )
    threshold = 0.5 * math.sqrt(fragments * rows * shards * cols)
    coef_ref[0] = jnp.minimum(1.0, threshold * lax.rsqrt(square_sum + 1e-06))

    for k in range(1, shards):
        square_copy(shard, lax.rem(shard + k, shards)).wait_send()
    for k in range(1, replicas):
        code_copy(rep, lax.rem(rep + k, replicas)).wait_send()


def update(
    p_ref,
    g_ref,
    m_ref,
    v_ref,
    coef_ref,
    global_ref,
    momentum_ref,
    p_hbm,
    m_hbm,
    v_hbm,
    global_hbm,
    momentum_hbm,
    p_out,
    m_out,
    v_out,
    outer_sems,
    sems,
):
    outer = [
        pltpu.make_async_copy(global_ref, global_hbm, outer_sems.at[0]),
        pltpu.make_async_copy(momentum_ref, momentum_hbm, outer_sems.at[1]),
    ]
    for copy in outer:
        copy.start()
    clip, rate_one, inv_two, chosen = (coef_ref[i, :1] for i in range(4))
    copies = []
    for f in range(p_ref.shape[1]):
        keep = jnp.where(chosen == f, 0.5, 1.0)
        scaled = g_ref[0, f].astype(jnp.float32) * clip
        first = 0.9 * m_ref[0, f] + 0.1 * scaled
        m_out[0, f] = first
        second = 0.95 * v_ref[0, f] + 0.05 * scaled * scaled
        v_out[0, f] = second
        unbiased = second * inv_two
        root = unbiased * lax.rsqrt(unbiased)
        stepped = 0.99 * p_ref[0, f] - first * rate_one / (root + 1e-08)
        p_out[0, f] = keep * stepped + (1.0 - keep) * global_ref[...]
        for i, (src, dst) in enumerate(((m_out, m_hbm), (v_out, v_hbm), (p_out, p_hbm))):
            copy = pltpu.make_async_copy(src.at[0, f], dst.at[0, f], sems.at[i, f])
            copy.start()
            copies.append(copy)
    for copy in outer + copies:
        copy.wait()


def local(replicas, shards, p, g, m, v, global_params, outer_momentum, fragment_index, step_count):
    rows, cols = global_params.shape
    fragments = p.shape[1]
    f32 = jnp.float32
    hbm = pl.BlockSpec(memory_space=pltpu.HBM)
    vmem = pl.BlockSpec(memory_space=pltpu.VMEM)
    held_rows = rows + rows // cols * SCALE_ROWS
    reader = min(1, shards - 1)
    said = lax.cond(
        lax.axis_index("fsdp") == reader,
        pl.pallas_call(
            read,
            out_shape=pltpu.VMEM((1, cols), f32),
            in_specs=[pl.BlockSpec(memory_space=pltpu.SMEM)],
            out_specs=vmem,
            name="read",
        ),
        lambda _: jnp.zeros((1, cols), f32),
        step_count,
    )
    held = pl.pallas_call(
        functools.partial(exchange, replicas, shards, reader),
        out_shape=(
            pltpu.VMEM(p.shape, p.dtype),
            pltpu.VMEM(g.shape, g.dtype),
            pltpu.VMEM(m.shape, m.dtype),
            pltpu.VMEM(v.shape, v.dtype),
            pltpu.VMEM((4, SUBLANES, cols), f32),
            pltpu.VMEM((rows, cols), f32),
            pltpu.VMEM((rows, cols), f32),
        ),
        in_specs=[pl.BlockSpec(memory_space=pltpu.SMEM), vmem] + [hbm] * 6,
        out_specs=(vmem,) * 7,
        scratch_shapes=[
            pltpu.VMEM((rows, cols), f32),
            pltpu.VMEM((rows, cols), f32),
            pltpu.VMEM((replicas, held_rows, cols), jnp.bfloat16),
            pltpu.VMEM((shards, 2, cols), f32),
            pltpu.SemaphoreType.DMA((6,)),
            pltpu.SemaphoreType.DMA((replicas,)),
            pltpu.SemaphoreType.DMA((replicas,)),
            pltpu.SemaphoreType.DMA((shards,)),
            pltpu.SemaphoreType.DMA((shards,)),
            pltpu.SemaphoreType.REGULAR((replicas,)),
            pltpu.SemaphoreType.REGULAR((shards,)),
        ],
        compiler_params=pltpu.CompilerParams(
            collective_id=0, has_side_effects=True, vmem_limit_bytes=16 * 1024 * 1024
        ),
        name="exchange",
    )(
        fragment_index,
        said,
        *(
            pltpu.with_memory_space_constraint(x, pltpu.HBM)
            for x in (p, g, m, v, global_params, outer_momentum)
        ),
    )
    return pl.pallas_call(
        update,
        out_shape=(
            jax.ShapeDtypeStruct(p.shape, f32),
            jax.ShapeDtypeStruct(m.shape, f32),
            jax.ShapeDtypeStruct(v.shape, f32),
            jax.ShapeDtypeStruct((rows, cols), f32),
            jax.ShapeDtypeStruct((rows, cols), f32),
        ),
        in_specs=[vmem] * 7,
        out_specs=(hbm,) * 5,
        scratch_shapes=[
            pltpu.VMEM(p.shape, f32),
            pltpu.VMEM(m.shape, f32),
            pltpu.VMEM(v.shape, f32),
            pltpu.SemaphoreType.DMA((2,)),
            pltpu.SemaphoreType.DMA((3, fragments)),
        ],
        compiler_params=pltpu.CompilerParams(vmem_limit_bytes=16 * 1024 * 1024),
        name="update",
    )(*held)


def solution(mesh):
    split = P("rep", None, "fsdp", None)
    outer = P("fsdp", None)
    return jax.shard_map(
        functools.partial(local, mesh.shape["rep"], mesh.shape["fsdp"]),
        mesh=mesh,
        in_specs=(split,) * 4 + (outer,) * 2 + (P(),) * 2,
        out_specs=(split,) * 3 + (outer,) * 2,
        check_vma=False,
    )
```

```python
import functools
import math

import jax
import jax.numpy as jnp
from jax import lax
from jax.experimental import pallas as pl
from jax.experimental.pallas import tpu as pltpu
from jax.sharding import PartitionSpec as P

MESH = pl.DeviceIdType.MESH
SUBLANES = 8
SCALE_ROWS = 16


def read(scalar_ref, said_ref):
    said_ref[...] = jnp.full(said_ref.shape, scalar_ref[0].astype(jnp.float32), jnp.float32)


def exchange(
    replicas,
    shards,
    reader,
    said_ref,
    p_hbm,
    g_hbm,
    m_hbm,
    v_hbm,
    gp_hbm,
    om_hbm,
    p_ref,
    g_ref,
    m_ref,
    v_ref,
    coef_ref,
    global_ref,
    momentum_ref,
    gp_ref,
    om_ref,
    coded,
    squares,
    told_ref,
    told_sems,
    load_sems,
    code_send,
    code_recv,
    square_send,
    square_recv,
    code_credit,
    square_credit,
):
    rep = lax.axis_index("rep")
    shard = lax.axis_index("fsdp")
    rows, cols = gp_ref.shape
    fragments = p_ref.shape[1]
    tells = lax.rem(shard, 2) == 1

    loads = [
        pltpu.make_async_copy(src, dst, load_sems.at[i])
        for i, (src, dst) in enumerate(
            (
                (g_hbm, g_ref),
                (gp_hbm, gp_ref),
                (p_hbm, p_ref),
                (om_hbm, om_ref),
                (m_hbm, m_ref),
                (v_hbm, v_ref),
            )
        )
    ]

    def higher(index, size, act):
        for k in range(1, size):

            @pl.when(index + k < size)
            def _():
                act(index + k)

    def lower(index, size, act):
        for k in range(size - 1, 0, -1):

            @pl.when(index - k >= 0)
            def _():
                act(index - k)

    def signal(sem, **target):
        pl.semaphore_signal(sem, inc=1, device_id=target, device_id_type=MESH)

    def square_copy(source, target):
        return pltpu.make_async_remote_copy(
            src_ref=squares.at[source],
            dst_ref=squares.at[source],
            send_sem=square_send.at[target],
            recv_sem=square_recv.at[source],
            device_id={"fsdp": target},
            device_id_type=MESH,
        )

    def code_copy(source, target):
        return pltpu.make_async_remote_copy(
            src_ref=coded.at[source],
            dst_ref=coded.at[source],
            send_sem=code_send.at[target],
            recv_sem=code_recv.at[source],
            device_id={"rep": target},
            device_id_type=MESH,
        )

    told_copy = pltpu.make_async_remote_copy(
        src_ref=said_ref,
        dst_ref=told_ref,
        send_sem=told_sems.at[0],
        recv_sem=told_sems.at[1],
        device_id={"fsdp": shard + 1 - 2 * lax.rem(shard, 2)},
        device_id_type=MESH,
    )

    barrier = pltpu.get_barrier_semaphore()
    for load in loads[:3]:
        load.start()
    higher(shard, shards, lambda i: signal(barrier, fsdp=i))
    higher(rep, replicas, lambda i: signal(barrier, rep=i))

    @pl.when(shard + rep > 0)
    def _():
        pl.semaphore_wait(barrier, shard + rep)

    @pl.when(tells)
    def _():
        told_copy.start()
        told_ref[...] = said_ref[...]

    lower(shard, shards, lambda i: signal(square_credit.at[shard], fsdp=i))
    lower(rep, replicas, lambda i: signal(code_credit.at[rep], rep=i))

    eye = lax.broadcasted_iota(jnp.int32, (cols, cols), 0) == lax.broadcasted_iota(
        jnp.int32, (cols, cols), 1
    )

    squares[shard, 1:] = said_ref[...]
    loads[0].wait()
    total = jnp.zeros((SUBLANES, cols), jnp.float32)
    for f in range(fragments):
        grad = g_ref[0, f].astype(jnp.float32)
        total = total + jnp.sum((grad * grad).reshape(-1, SUBLANES, cols), axis=0)
    squares[shard, :1] = jnp.sum(total, axis=0, keepdims=True)
    lower(shard, shards, lambda i: square_copy(shard, i).start())

    def square_when_heard(i):
        pl.semaphore_wait(square_credit.at[i], 1)
        square_copy(shard, i).start()

    @pl.when(jnp.logical_not(tells))
    def _():
        told_copy.wait_recv()

    told = told_ref[...]

    for load in loads[1:3]:
        load.wait()
    for load in loads[3:]:
        load.start()
    chosen = p_ref[0, 0]
    for f in range(1, fragments):
        chosen = jnp.where(told == f, p_ref[0, f], chosen)
    pseudo = gp_ref[...] - chosen
    scale = (jnp.max(jnp.abs(pseudo), axis=1, keepdims=True) + 1e-06).astype(jnp.bfloat16)
    scale = scale.astype(jnp.float32)
    coded[rep, :rows] = (pseudo / scale).astype(jnp.bfloat16)
    for c in range(rows // cols):
        column = scale[c * cols : (c + 1) * cols]
        line = jnp.sum(jnp.where(eye, column, 0.0), axis=0, keepdims=True)
        coded[rep, rows + c * SCALE_ROWS : rows + (c + 1) * SCALE_ROWS] = jnp.broadcast_to(
            line, (SCALE_ROWS, cols)
        ).astype(jnp.bfloat16)

    def code_when_heard(i):
        pl.semaphore_wait(code_credit.at[i], 1)
        code_copy(rep, i).start()

    lower(rep, replicas, lambda i: code_copy(rep, i).start())
    higher(rep, replicas, code_when_heard)
    higher(shard, shards, square_when_heard)
    coef_ref[3] = jnp.broadcast_to(told, (SUBLANES, cols))
    for load in loads[3:]:
        load.wait()

    summed = [jnp.zeros((cols, cols), jnp.float32)] * (rows // cols)
    for r in range(replicas):

        @pl.when(rep != r)
        def _():
            code_copy(r, r).wait_recv()

        for c in range(rows // cols):
            line = coded[r, rows + c * SCALE_ROWS : rows + (c + 1) * SCALE_ROWS]
            line = line.astype(jnp.float32)[:1]
            column = jnp.sum(jnp.where(eye, line, 0.0), axis=1, keepdims=True)
            summed[c] = summed[c] + coded[r, c * cols : (c + 1) * cols].astype(jnp.float32) * column
    for c in range(rows // cols):
        part = slice(c * cols, (c + 1) * cols)
        averaged = summed[c] * (1.0 / replicas)
        momentum = 0.9 * om_ref[part] + averaged
        momentum_ref[part] = momentum
        global_ref[part] = gp_ref[part] - 0.7 * (averaged + 0.9 * momentum)

    def square_heard(source):
        @pl.when(shard != source)
        def _():
            square_copy(source, source).wait_recv()

    square_heard(reader)
    step = jnp.broadcast_to(squares[reader, 1:], (SUBLANES, cols))
    coef_ref[1] = 0.1 / (1.0 - jnp.exp(step * math.log(0.9)))
    coef_ref[2] = 1.0 / (1.0 - jnp.exp(step * math.log(0.95)))
    for s in range(shards):
        if s != reader:
            square_heard(s)
    lanes = squares[0, :1]
    for s in range(1, shards):
        lanes = lanes + squares[s, :1]
    square_sum = jnp.broadcast_to(
        jnp.sum(jnp.broadcast_to(lanes, (SUBLANES, cols)), axis=1, keepdims=True),
        (SUBLANES, cols),
    )
    threshold = 0.5 * math.sqrt(fragments * rows * shards * cols)
    coef_ref[0] = jnp.minimum(1.0, threshold * lax.rsqrt(square_sum + 1e-06))

    for k in range(1, shards):
        square_copy(shard, lax.rem(shard + k, shards)).wait_send()
    for k in range(1, replicas):
        code_copy(rep, lax.rem(rep + k, replicas)).wait_send()

    @pl.when(tells)
    def _():
        told_copy.wait_send()


def update(
    p_ref,
    g_ref,
    m_ref,
    v_ref,
    coef_ref,
    global_ref,
    momentum_ref,
    p_hbm,
    m_hbm,
    v_hbm,
    global_hbm,
    momentum_hbm,
    p_out,
    m_out,
    v_out,
    outer_sems,
    sems,
):
    outer = [
        pltpu.make_async_copy(global_ref, global_hbm, outer_sems.at[0]),
        pltpu.make_async_copy(momentum_ref, momentum_hbm, outer_sems.at[1]),
    ]
    for copy in outer:
        copy.start()
    clip, rate_one, inv_two, chosen = (coef_ref[i, :1] for i in range(4))
    copies = []
    for f in range(p_ref.shape[1]):
        keep = jnp.where(chosen == f, 0.5, 1.0)
        scaled = g_ref[0, f].astype(jnp.float32) * clip
        first = 0.9 * m_ref[0, f] + 0.1 * scaled
        m_out[0, f] = first
        second = 0.95 * v_ref[0, f] + 0.05 * scaled * scaled
        v_out[0, f] = second
        unbiased = second * inv_two
        root = unbiased * lax.rsqrt(unbiased)
        stepped = 0.99 * p_ref[0, f] - first * rate_one / (root + 1e-08)
        p_out[0, f] = keep * stepped + (1.0 - keep) * global_ref[...]
        for i, (src, dst) in enumerate(((m_out, m_hbm), (v_out, v_hbm), (p_out, p_hbm))):
            copy = pltpu.make_async_copy(src.at[0, f], dst.at[0, f], sems.at[i, f])
            copy.start()
            copies.append(copy)
    for copy in outer + copies:
        copy.wait()


def local(replicas, shards, p, g, m, v, global_params, outer_momentum, fragment_index, step_count):
    rows, cols = global_params.shape
    fragments = p.shape[1]
    f32 = jnp.float32
    hbm = pl.BlockSpec(memory_space=pltpu.HBM)
    vmem = pl.BlockSpec(memory_space=pltpu.VMEM)
    held_rows = rows + rows // cols * SCALE_ROWS
    assert shards % 2 == 0
    reader = 2 % shards
    shard = lax.axis_index("fsdp")
    speak = pl.pallas_call(
        read,
        out_shape=pltpu.VMEM((1, cols), f32),
        in_specs=[pl.BlockSpec(memory_space=pltpu.SMEM)],
        out_specs=vmem,
        name="read",
    )
    said = lax.switch(
        jnp.where(shard % 2 == 1, 0, jnp.where(shard == reader, 1, 2)),
        (
            lambda frag, step: speak(frag),
            lambda frag, step: speak(step),
            lambda frag, step: jnp.zeros((1, cols), f32),
        ),
        fragment_index,
        step_count,
    )
    held = pl.pallas_call(
        functools.partial(exchange, replicas, shards, reader),
        out_shape=(
            pltpu.VMEM(p.shape, p.dtype),
            pltpu.VMEM(g.shape, g.dtype),
            pltpu.VMEM(m.shape, m.dtype),
            pltpu.VMEM(v.shape, v.dtype),
            pltpu.VMEM((4, SUBLANES, cols), f32),
            pltpu.VMEM((rows, cols), f32),
            pltpu.VMEM((rows, cols), f32),
        ),
        in_specs=[vmem] + [hbm] * 6,
        out_specs=(vmem,) * 7,
        scratch_shapes=[
            pltpu.VMEM((rows, cols), f32),
            pltpu.VMEM((rows, cols), f32),
            pltpu.VMEM((replicas, held_rows, cols), jnp.bfloat16),
            pltpu.VMEM((shards, 2, cols), f32),
            pltpu.VMEM((1, cols), f32),
            pltpu.SemaphoreType.DMA((2,)),
            pltpu.SemaphoreType.DMA((6,)),
            pltpu.SemaphoreType.DMA((replicas,)),
            pltpu.SemaphoreType.DMA((replicas,)),
            pltpu.SemaphoreType.DMA((shards,)),
            pltpu.SemaphoreType.DMA((shards,)),
            pltpu.SemaphoreType.REGULAR((replicas,)),
            pltpu.SemaphoreType.REGULAR((shards,)),
        ],
        compiler_params=pltpu.CompilerParams(
            collective_id=0, has_side_effects=True, vmem_limit_bytes=16 * 1024 * 1024
        ),
        name="exchange",
    )(
        said,
        *(
            pltpu.with_memory_space_constraint(x, pltpu.HBM)
            for x in (p, g, m, v, global_params, outer_momentum)
        ),
    )
    return pl.pallas_call(
        update,
        out_shape=(
            jax.ShapeDtypeStruct(p.shape, f32),
            jax.ShapeDtypeStruct(m.shape, f32),
            jax.ShapeDtypeStruct(v.shape, f32),
            jax.ShapeDtypeStruct((rows, cols), f32),
            jax.ShapeDtypeStruct((rows, cols), f32),
        ),
        in_specs=[vmem] * 7,
        out_specs=(hbm,) * 5,
        scratch_shapes=[
            pltpu.VMEM(p.shape, f32),
            pltpu.VMEM(m.shape, f32),
            pltpu.VMEM(v.shape, f32),
            pltpu.SemaphoreType.DMA((2,)),
            pltpu.SemaphoreType.DMA((3, fragments)),
        ],
        compiler_params=pltpu.CompilerParams(vmem_limit_bytes=16 * 1024 * 1024),
        name="update",
    )(*held)


def solution(mesh):
    split = P("rep", None, "fsdp", None)
    outer = P("fsdp", None)
    return jax.shard_map(
        functools.partial(local, mesh.shape["rep"], mesh.shape["fsdp"]),
        mesh=mesh,
        in_specs=(split,) * 4 + (outer,) * 2 + (P(),) * 2,
        out_specs=(split,) * 3 + (outer,) * 2,
        check_vma=False,
    )
```

```python
import functools
import math

import jax
import jax.numpy as jnp
from jax import lax
from jax.experimental import pallas as pl
from jax.experimental.pallas import tpu as pltpu
from jax.sharding import PartitionSpec as P

MESH = pl.DeviceIdType.MESH
SUBLANES = 8
SCALE_ROWS = 16


def read(scalar_ref, said_ref):
    said_ref[...] = jnp.full(said_ref.shape, scalar_ref[0].astype(jnp.float32), jnp.float32)


def exchange(
    replicas,
    shards,
    reader,
    said_ref,
    p_hbm,
    g_hbm,
    m_hbm,
    v_hbm,
    gp_hbm,
    om_hbm,
    p_ref,
    g_ref,
    m_ref,
    v_ref,
    coef_ref,
    global_ref,
    momentum_ref,
    gp_ref,
    om_ref,
    coded,
    squares,
    told_ref,
    told_sems,
    load_sems,
    code_send,
    code_recv,
    square_send,
    square_recv,
    code_credit,
    square_credit,
):
    rep = lax.axis_index("rep")
    shard = lax.axis_index("fsdp")
    rows, cols = gp_ref.shape
    fragments = p_ref.shape[1]
    pair = shard // 2
    tells = lax.rem(shard, 2) == 1

    loads = [
        pltpu.make_async_copy(src, dst, load_sems.at[i])
        for i, (src, dst) in enumerate(
            (
                (g_hbm, g_ref),
                (gp_hbm, gp_ref),
                (p_hbm, p_ref),
                (om_hbm, om_ref),
                (m_hbm, m_ref),
                (v_hbm, v_ref),
            )
        )
    ]

    def higher(index, size, act):
        for k in range(1, size):

            @pl.when(index + k < size)
            def _():
                act(index + k)

    def lower(index, size, act):
        for k in range(size - 1, 0, -1):

            @pl.when(index - k >= 0)
            def _():
                act(index - k)

    def signal(sem, **target):
        pl.semaphore_signal(sem, inc=1, device_id=target, device_id_type=MESH)

    def square_copy(source, target):
        return pltpu.make_async_remote_copy(
            src_ref=squares.at[source],
            dst_ref=squares.at[source],
            send_sem=square_send,
            recv_sem=square_recv,
            device_id={"fsdp": target},
            device_id_type=MESH,
        )

    def code_copy(source, target):
        return pltpu.make_async_remote_copy(
            src_ref=coded.at[source],
            dst_ref=coded.at[source],
            send_sem=code_send,
            recv_sem=code_recv.at[source],
            device_id={"rep": target},
            device_id_type=MESH,
        )

    told_copy = pltpu.make_async_remote_copy(
        src_ref=said_ref,
        dst_ref=told_ref,
        send_sem=told_sems.at[0],
        recv_sem=told_sems.at[1],
        device_id={"fsdp": shard + 1 - 2 * lax.rem(shard, 2)},
        device_id_type=MESH,
    )

    barrier = pltpu.get_barrier_semaphore()
    for load in loads[:3]:
        load.start()
    higher(shard, shards, lambda i: signal(barrier, fsdp=i))
    higher(rep, replicas, lambda i: signal(barrier, rep=i))

    @pl.when(shard + rep > 0)
    def _():
        pl.semaphore_wait(barrier, shard + rep)

    @pl.when(tells)
    def _():
        told_copy.start()
        told_ref[...] = said_ref[...]

    lower(shard, shards, lambda i: signal(square_credit.at[pair], fsdp=i))
    lower(rep, replicas, lambda i: signal(code_credit, rep=i))

    eye = lax.broadcasted_iota(jnp.int32, (cols, cols), 0) == lax.broadcasted_iota(
        jnp.int32, (cols, cols), 1
    )

    squares[shard, 1:] = said_ref[...]
    loads[0].wait()
    total = jnp.zeros((SUBLANES, cols), jnp.float32)
    for f in range(fragments):
        grad = g_ref[0, f].astype(jnp.float32)
        total = total + jnp.sum((grad * grad).reshape(-1, SUBLANES, cols), axis=0)
    squares[shard, :1] = jnp.sum(total, axis=0, keepdims=True)
    lower(shard, shards, lambda i: square_copy(shard, i).start())

    @pl.when(jnp.logical_not(tells))
    def _():
        told_copy.wait_recv()

    told = told_ref[...]

    for load in loads[1:3]:
        load.wait()
    for load in loads[3:]:
        load.start()
    chosen = p_ref[0, 0]
    for f in range(1, fragments):
        chosen = jnp.where(told == f, p_ref[0, f], chosen)
    pseudo = gp_ref[...] - chosen
    scale = (jnp.max(jnp.abs(pseudo), axis=1, keepdims=True) + 1e-06).astype(jnp.bfloat16)
    scale = scale.astype(jnp.float32)
    coded[rep, :rows] = (pseudo / scale).astype(jnp.bfloat16)
    for c in range(rows // cols):
        column = scale[c * cols : (c + 1) * cols]
        line = jnp.sum(jnp.where(eye, column, 0.0), axis=0, keepdims=True)
        coded[rep, rows + c * SCALE_ROWS : rows + (c + 1) * SCALE_ROWS] = jnp.broadcast_to(
            line, (SCALE_ROWS, cols)
        ).astype(jnp.bfloat16)

    lower(rep, replicas, lambda i: code_copy(rep, i).start())

    @pl.when(rep + 1 < replicas)
    def _():
        pl.semaphore_wait(code_credit, replicas - 1 - rep)

    higher(rep, replicas, lambda i: code_copy(rep, i).start())

    @pl.when(jnp.logical_not(tells))
    def _():
        pl.semaphore_wait(square_credit.at[pair], 1)
        square_copy(shard, shard + 1).start()

    def squares_when_heard(chip):
        pl.semaphore_wait(square_credit.at[chip], 2)
        square_copy(shard, 2 * chip).start()
        square_copy(shard, 2 * chip + 1).start()

    higher(pair, shards // 2, squares_when_heard)
    coef_ref[3] = jnp.broadcast_to(told, (SUBLANES, cols))
    for load in loads[3:]:
        load.wait()

    summed = [jnp.zeros((cols, cols), jnp.float32)] * (rows // cols)
    for r in range(replicas):

        @pl.when(rep != r)
        def _():
            code_copy(r, r).wait_recv()

        for c in range(rows // cols):
            line = coded[r, rows + c * SCALE_ROWS : rows + (c + 1) * SCALE_ROWS]
            line = line.astype(jnp.float32)[:1]
            column = jnp.sum(jnp.where(eye, line, 0.0), axis=1, keepdims=True)
            summed[c] = summed[c] + coded[r, c * cols : (c + 1) * cols].astype(jnp.float32) * column
    for c in range(rows // cols):
        part = slice(c * cols, (c + 1) * cols)
        averaged = summed[c] * (1.0 / replicas)
        momentum = 0.9 * om_ref[part] + averaged
        momentum_ref[part] = momentum
        global_ref[part] = gp_ref[part] - 0.7 * (averaged + 0.9 * momentum)

    others = squares.at[pl.ds(0, shards - 1)]
    pltpu.make_async_copy(others, others, square_recv).wait()
    step = jnp.broadcast_to(squares[reader, 1:], (SUBLANES, cols))
    coef_ref[1] = 0.1 / (1.0 - jnp.exp(step * math.log(0.9)))
    coef_ref[2] = 1.0 / (1.0 - jnp.exp(step * math.log(0.95)))
    lanes = squares[0, :1]
    for s in range(1, shards):
        lanes = lanes + squares[s, :1]
    square_sum = jnp.broadcast_to(
        jnp.sum(jnp.broadcast_to(lanes, (SUBLANES, cols)), axis=1, keepdims=True),
        (SUBLANES, cols),
    )
    threshold = 0.5 * math.sqrt(fragments * rows * shards * cols)
    coef_ref[0] = jnp.minimum(1.0, threshold * lax.rsqrt(square_sum + 1e-06))

    pltpu.make_async_copy(others, others, square_send).wait()
    sent = coded.at[pl.ds(0, replicas - 1)]
    pltpu.make_async_copy(sent, sent, code_send).wait()

    @pl.when(tells)
    def _():
        told_copy.wait_send()


def update(
    p_ref,
    g_ref,
    m_ref,
    v_ref,
    coef_ref,
    global_ref,
    momentum_ref,
    p_hbm,
    m_hbm,
    v_hbm,
    global_hbm,
    momentum_hbm,
    p_out,
    m_out,
    v_out,
    outer_sems,
    sems,
):
    outer = [
        pltpu.make_async_copy(global_ref, global_hbm, outer_sems.at[0]),
        pltpu.make_async_copy(momentum_ref, momentum_hbm, outer_sems.at[1]),
    ]
    for copy in outer:
        copy.start()
    clip, rate_one, inv_two, chosen = (coef_ref[i, :1] for i in range(4))
    for f in range(p_ref.shape[1]):
        keep = jnp.where(chosen == f, 0.5, 1.0)
        scaled = g_ref[0, f].astype(jnp.float32) * clip
        first = 0.9 * m_ref[0, f] + 0.1 * scaled
        m_out[0, f] = first
        second = 0.95 * v_ref[0, f] + 0.05 * scaled * scaled
        v_out[0, f] = second
        unbiased = second * inv_two
        root = unbiased * lax.rsqrt(unbiased)
        stepped = 0.99 * p_ref[0, f] - first * rate_one / (root + 1e-08)
        p_out[0, f] = keep * stepped + (1.0 - keep) * global_ref[...]
        for i, (src, dst) in enumerate(((m_out, m_hbm), (v_out, v_hbm), (p_out, p_hbm))):
            copy = pltpu.make_async_copy(src.at[0, f], dst.at[0, f], sems.at[i])
            copy.start()
    for i, (src, dst) in enumerate(((m_out, m_hbm), (v_out, v_hbm), (p_out, p_hbm))):
        pltpu.make_async_copy(src, dst, sems.at[i]).wait()
    for copy in outer:
        copy.wait()


def local(replicas, shards, p, g, m, v, global_params, outer_momentum, fragment_index, step_count):
    rows, cols = global_params.shape
    fragments = p.shape[1]
    f32 = jnp.float32
    hbm = pl.BlockSpec(memory_space=pltpu.HBM)
    vmem = pl.BlockSpec(memory_space=pltpu.VMEM)
    held_rows = rows + rows // cols * SCALE_ROWS
    assert shards % 2 == 0
    reader = 2 % shards
    shard = lax.axis_index("fsdp")
    speak = pl.pallas_call(
        read,
        out_shape=pltpu.VMEM((1, cols), f32),
        in_specs=[pl.BlockSpec(memory_space=pltpu.SMEM)],
        out_specs=vmem,
        name="read",
    )
    said = lax.switch(
        jnp.where(shard % 2 == 1, 0, jnp.where(shard == reader, 1, 2)),
        (
            lambda frag, step: speak(frag),
            lambda frag, step: speak(step),
            lambda frag, step: jnp.zeros((1, cols), f32),
        ),
        fragment_index,
        step_count,
    )
    held = pl.pallas_call(
        functools.partial(exchange, replicas, shards, reader),
        out_shape=(
            pltpu.VMEM(p.shape, p.dtype),
            pltpu.VMEM(g.shape, g.dtype),
            pltpu.VMEM(m.shape, m.dtype),
            pltpu.VMEM(v.shape, v.dtype),
            pltpu.VMEM((4, SUBLANES, cols), f32),
            pltpu.VMEM((rows, cols), f32),
            pltpu.VMEM((rows, cols), f32),
        ),
        in_specs=[vmem] + [hbm] * 6,
        out_specs=(vmem,) * 7,
        scratch_shapes=[
            pltpu.VMEM((rows, cols), f32),
            pltpu.VMEM((rows, cols), f32),
            pltpu.VMEM((replicas, held_rows, cols), jnp.bfloat16),
            pltpu.VMEM((shards, 2, cols), f32),
            pltpu.VMEM((1, cols), f32),
            pltpu.SemaphoreType.DMA((2,)),
            pltpu.SemaphoreType.DMA((6,)),
            pltpu.SemaphoreType.DMA,
            pltpu.SemaphoreType.DMA((replicas,)),
            pltpu.SemaphoreType.DMA,
            pltpu.SemaphoreType.DMA,
            pltpu.SemaphoreType.REGULAR,
            pltpu.SemaphoreType.REGULAR((shards // 2,)),
        ],
        compiler_params=pltpu.CompilerParams(
            collective_id=0, has_side_effects=True, vmem_limit_bytes=16 * 1024 * 1024
        ),
        name="exchange",
    )(
        said,
        *(
            pltpu.with_memory_space_constraint(x, pltpu.HBM)
            for x in (p, g, m, v, global_params, outer_momentum)
        ),
    )
    return pl.pallas_call(
        update,
        out_shape=(
            jax.ShapeDtypeStruct(p.shape, f32),
            jax.ShapeDtypeStruct(m.shape, f32),
            jax.ShapeDtypeStruct(v.shape, f32),
            jax.ShapeDtypeStruct((rows, cols), f32),
            jax.ShapeDtypeStruct((rows, cols), f32),
        ),
        in_specs=[vmem] * 7,
        out_specs=(hbm,) * 5,
        scratch_shapes=[
            pltpu.VMEM(p.shape, f32),
            pltpu.VMEM(m.shape, f32),
            pltpu.VMEM(v.shape, f32),
            pltpu.SemaphoreType.DMA((2,)),
            pltpu.SemaphoreType.DMA((3,)),
        ],
        compiler_params=pltpu.CompilerParams(vmem_limit_bytes=16 * 1024 * 1024),
        name="update",
    )(*held)


def solution(mesh):
    split = P("rep", None, "fsdp", None)
    outer = P("fsdp", None)
    return jax.shard_map(
        functools.partial(local, mesh.shape["rep"], mesh.shape["fsdp"]),
        mesh=mesh,
        in_specs=(split,) * 4 + (outer,) * 2 + (P(),) * 2,
        out_specs=(split,) * 3 + (outer,) * 2,
        check_vma=False,
    )
```
